512 devices in a mesh: section: 8 (over x, core), expert: 64 (over y, z).
Axes of the slice: x: 4, y: 4, z: 16, core: 2. Of those that a mesh axis runs over, the one named last changes fastest.
Arguments:
- tokens: bfloat16 [8192, 4096], P('expert', 'section'), may hold values from -6 to 6
- expert_ids: int32 [8192, 8], P('expert'), may hold values from 0 to 63, all different within a row; in each aligned block of 128 rows (0 to 127, 128 to 255, ...) at most 20 rows name the same one
- numerators: int32 [8192, 8], P('expert'), may hold values from 1 to 255
- gate_up_weight: bfloat16 [64, 4096, 3072], P('expert', None, 'section'), may hold values from -0.09375 to 0.09375
- down_weight: bfloat16 [64, 1536, 4096], P('expert', None, 'section'), may hold values from -0.15625 to 0.15625
Outputs:
- mixed: bfloat16 [8192, 4096], P('expert', 'section')
The draws below stay inside these ranges and needn't reach their ends.
Inputs may be any that keep to these rules, and one draw needn't show every extreme that they name: `expert_ids`: each row names 8 different experts. Among the rows of one index of expert (aligned blocks of 128 rows) no expert is named more than 20 times, and in every draw some expert is named exactly 20 times there.
All inputs are finite; a program needn't handle non-finite values.
Results may differ from the reference program's by a relative error of at most 0.0057.
Values may be sent and summed in bfloat16 or wider, within the bound.
A program may use at most 128 MiB of HBM per device.

```python
import math
import jax
import jax.numpy as jnp
import numpy as np
from jax import lax

D = 4096
FF = 1536
BLOCK_UNITS = 64
TOPK = 8
TOK_DEV = 128
EXPERTS = 64
TOKENS = 8192
CAP = 20


def set_ends(values, own_key, least, top_value):
    longest = values.shape.index(max(values.shape))
    spots = []
    for shift in (0, 1):
        where = [jax.random.randint(jax.random.fold_in(own_key, axis), (), 0, length) for axis, length in enumerate(values.shape)]
        where[longest] = (where[longest] + shift) % values.shape[longest]
        spots.append(tuple(where))
    return values.at[spots[0]].set(least).at[spots[1]].set(top_value)


def shard_levels(own_key, extent, split, least, largest):
    factor_of = 1.0
    for axis_at, shards_of in split:
        steps = jax.random.uniform(jax.random.fold_in(jax.random.fold_in(own_key, 6), axis_at), (shards_of,), jnp.float32, least / len(split), largest / len(split))
        factor_of = factor_of * jnp.repeat(jnp.exp(steps), extent[axis_at] // shards_of).reshape((-1,) + (1,) * (len(extent) - 1 - axis_at))
    return factor_of


def shared_out(stream_key, own, number, rows, count, top, reach, skew):
    order = jax.random.permutation(stream_key, count)
    crowded, common = load_shares(count, rows * top, reach, skew, True), load_shares(count, rows * top, reach, skew, False)
    places = jnp.arange(count)

    def named(tallies, rotation):
        used = int((tallies > 0).sum())
        fixed = max(1, used // 4)
        passed = fixed + (places - fixed + rotation * (used - fixed)) % max(1, count - fixed)
        return jnp.zeros((count,), jnp.int32).at[order[jnp.where(places < fixed, places, passed)]].set(jnp.asarray(tallies, jnp.int32))

    tallies = jnp.where(number % 4 == 0, named(crowded, number // 4), named(common, number - number // 4 - 1))
    mixed = jax.random.permutation(jax.random.fold_in(own, 3), count)
    giver, taker = mixed[0:count // 2 * 2:2], mixed[1:count // 2 * 2:2]
    margin = jnp.minimum(tallies[giver] - 1, reach - tallies[taker]) // 2
    margin = jnp.where((giver == order[0]) | (taker == order[0]) | (tallies[taker] == 0), 0, jnp.maximum(margin, 0))
    passed = jax.random.randint(jax.random.fold_in(own, 4), (count // 2,), 0, 1 << 20) % (margin + 1)
    tallies = tallies.at[giver].add(-passed).at[taker].add(passed)
    members = jnp.searchsorted(jnp.cumsum(tallies), jnp.arange(rows * top), side="right").astype(jnp.int32)
    grid = members.reshape(top, rows).T
    grid = grid[jax.random.permutation(jax.random.fold_in(own, 1), rows)]
    rotation = jax.random.randint(jax.random.fold_in(own, 2), (rows, 1), 0, top)
    return jnp.take_along_axis(grid, (jnp.arange(top)[None, :] + rotation) % top, axis=1)


def load_shares(amount, total, bound, slope, full):
    portions = [(1 << 20) // math.isqrt(standing ** slope) + 1 for standing in range(1, amount + 1)]
    largest = bound if full else min(bound, max(-(-total // amount), total * portions[0] // sum(portions)))
    least = 1 if total - largest >= amount - 1 else 0
    holding, surplus = [largest] + [least] * (amount - 1), total - largest - least * (amount - 1)
    while surplus > 0:
        candidates = [i for i in range(1, amount) if holding[i] < largest] or [i for i in range(1, amount) if holding[i] < bound]
        whole, remaining = sum([portions[i] for i in candidates]), surplus
        for i in candidates:
            extra = min(bound - holding[i], max(1, remaining * portions[i] // whole), surplus)
            holding[i] = holding[i] + extra
            surplus = surplus - extra
    return np.array(holding)


def gaussian(rng, dims, scale, bound, pieces=(), held_as=jnp.bfloat16):
    gain = shard_levels(rng, dims, pieces, -0.22, 0.18) if pieces else 1.0
    drawn = jax.random.normal(rng, dims, jnp.float32) * scale * gain
    return jnp.minimum(jnp.maximum(drawn, -bound), bound).astype(held_as)


def setup_inputs(seed: int = 0) -> dict:
    seeds = jax.random.split(jax.random.key(seed), 6)
    tokens = gaussian(seeds[0], (TOKENS, D), 1.0, 6.0, ((0, 64), (1, 8)))
    expert_ids_keys = jax.random.split(jax.random.fold_in(seeds[1], 1), TOKENS // TOK_DEV)
    expert_ids_turns = jax.random.permutation(jax.random.fold_in(seeds[1], 3), TOKENS // TOK_DEV)
    expert_ids = jax.vmap(lambda own, number: shared_out(jax.random.fold_in(seeds[1], 2), own, number, TOK_DEV, EXPERTS, TOPK, CAP, 2))(expert_ids_keys, expert_ids_turns).reshape((TOKENS, TOPK))
    numerators = set_ends(jax.random.randint(seeds[2], (TOKENS, TOPK), 1, 256), jax.random.fold_in(seeds[2], 1), 1, 255).astype(jnp.int32)
    gate_up_weight = gaussian(seeds[3], (EXPERTS, D, 2 * FF), D ** -0.5, 0.09375, ((0, 64), (2, 8)))
    down_weight = gaussian(seeds[4], (EXPERTS, FF, D), FF ** -0.5, 0.15625, ((0, 64), (2, 8)))
    return {"tokens": tokens, "expert_ids": expert_ids, "numerators": numerators, "gate_up_weight": gate_up_weight, "down_weight": down_weight}


denominator = 256.0


def reference(tokens, expert_ids, numerators, gate_up_weight, down_weight):
    blocks = TOKENS // TOK_DEV
    assigned = TOK_DEV * TOPK
    flat = expert_ids.reshape(blocks, assigned).astype(jnp.int32)
    hits = (flat[:, :, None] == jnp.arange(EXPERTS, dtype=jnp.int32)[None, None, :]).astype(jnp.int32)
    rank = jnp.sum((jnp.cumsum(hits, axis=1) - hits) * hits, axis=2).astype(jnp.int32)
    block_ids = jnp.arange(blocks, dtype=jnp.int32)[:, None]
    slot = (block_ids * CAP + rank).astype(jnp.int32)
    source = (block_ids * TOK_DEV + jnp.arange(assigned, dtype=jnp.int32)[None, :] // TOPK).astype(jnp.int32)
    table = jnp.full((EXPERTS, blocks * CAP), TOKENS, jnp.int32).at[flat, slot].set(source)
    weights = numerators.reshape(blocks, assigned).astype(jnp.float32) / denominator
    scales = jnp.zeros((EXPERTS, blocks * CAP), jnp.float32).at[flat, slot].set(weights)

    def one_expert(total, packed):
        index, scale, w_both, w_down = packed
        rows = jnp.take(tokens, index, axis=0, mode="fill", fill_value=0)
        both = jnp.dot(rows, w_both, preferred_element_type=jnp.float32)
        split_up = both.reshape(rows.shape[0], FF // BLOCK_UNITS, 2, BLOCK_UNITS)
        gate = split_up[:, :, 0, :].reshape(rows.shape[0], FF)
        up = split_up[:, :, 1, :].reshape(rows.shape[0], FF)
        hidden = (jax.nn.silu(gate) * up).astype(jnp.bfloat16)
        result = jnp.dot(hidden, w_down, preferred_element_type=jnp.float32).astype(jnp.bfloat16)
        total = total.at[index].add(result.astype(jnp.float32) * scale[:, None], mode="drop")
        return total, None

    start = jnp.zeros((TOKENS, D), jnp.float32)
    total, _ = lax.scan(one_expert, start, (table, scales, gate_up_weight, down_weight))
    return total.astype(jnp.bfloat16)
```

```python
import functools

import jax
import jax.numpy as jnp
from jax import lax
from jax.experimental import pallas as pl
from jax.experimental.pallas import tpu as pltpu
from jax.sharding import PartitionSpec as P

MESH = pl.DeviceIdType.MESH
BF = jnp.bfloat16
F32 = jnp.float32

NX, NY, NZ = 4, 4, 16
CAP = 20
GROUPS = ((6, -7, 7, -8), (4, -5, 5, -6), (2, -3, 3, -4), (0, -1, 1, -2))
PLACE = {off: (g, i) for g, offs in enumerate(GROUPS) for i, off in enumerate(offs)}
ORDER = (
    "A1", "A2", "S3", "A3", "Y3", "A4", "S2", "A5", "Y2", "A6", "S1", "X3",
    "A7", "Y1", "A8", "S0", "Z3", "Y0", "M3", "X2", "H3", "Z2", "I3", "M2",
    "J3", "H2", "N3", "X0", "I2", "Z0", "J2", "M0", "N2", "H0", "C3", "C2",
    "X1", "I0", "Z1", "J0", "M1", "N0", "H1", "C0", "R0", "R1", "I1", "J1",
    "N1", "C1", "R2", "R3", "R4", "R5", "R6", "R7",
)


def kernel(
    tok_in, route_in, wgu_hbm, wd_hbm, out_ref,
    tok, route, wgu, wd, wsel, ysend, xfull, acc1, hx_send, hx_recv, hfull, acc2, ret, back, part,
    dsend, usend, drecv, urecv,
    wg_sem, wd_sem, tok_s, tok_r, rt_s, rt_r, y_s, y_r, x_s, x_r, xc_s, xc_r,
    hx_s, hx_r, h_s, h_r, hc_s, hc_r, b_s, b_r, d_s, d_r, u_s, u_r,
):
    sec, exp = lax.axis_index("section"), lax.axis_index("expert")
    x, core = sec // 2, sec % 2
    y, z = exp // NZ, exp % NZ
    z_up = (sec, y * NZ + (z + 1) % NZ)
    z_dn = (sec, y * NZ + (z + NZ - 1) % NZ)
    y_at = [(sec, ((y + o) % NY) * NZ + z) for o in range(NY)]
    x_up = (((x + 1) % NX) * 2 + core, exp)
    x_dn = (((x + NX - 1) % NX) * 2 + core, exp)
    sib = (x * 2 + (1 - core), exp)
    peers = [z_up, z_dn, y_at[1], y_at[2], y_at[3], x_up, x_dn, sib]

    rows = NY * 4 * CAP
    quarter = 4 * CAP
    half = rows // 2
    feat = tok_in.shape[1]
    nsec = 2 * NX
    pend = []

    def remote(src, dst, ss, rs, dev):
        c = pltpu.make_async_remote_copy(
            src_ref=src, dst_ref=dst, send_sem=ss, recv_sem=rs, device_id=dev, device_id_type=MESH
        )
        c.start()
        pend.append(c)
        return c

    def landed(dst, rs):
        pltpu.make_async_remote_copy(
            src_ref=dst, dst_ref=dst, send_sem=rs, recv_sem=rs, device_id=sib, device_id_type=MESH
        ).wait_recv()

    for o in range(NX):
        for c in range(2):
            s = ((x + o) % NX) * 2 + (core + c) % 2
            pltpu.make_async_copy(
                wgu_hbm.at[0, pl.ds(pl.multiple_of(s * feat, feat), feat), :],
                wgu.at[o * 2 + c], wg_sem,
            ).start()
    units = wd_hbm.shape[1] // NX
    third = units // 6
    for o in range(NX):
        base = ((x + o) % NX) * units
        for frm, to, size in ((0, 0, 3), (5, 3, 1), (3, 4, 2)):
            pltpu.make_async_copy(
                wd_hbm.at[0, pl.ds(pl.multiple_of(base + frm * third, third), size * third), :],
                wd.at[o, pl.ds(to * third, size * third), :], wd_sem,
            ).start()

    barrier = pltpu.get_barrier_semaphore()
    for p in peers:
        pl.semaphore_signal(barrier, inc=1, device_id=p, device_id_type=MESH)
    pl.semaphore_wait(barrier, len(peers))

    def tslot(off):
        g, i = PLACE[off]
        return tok.at[g, pl.ds(i * 128, 128), :], route.at[g, i]

    def send_block(src, rsrc, off_there, dev):
        td, rd = tslot(off_there)
        k = off_there + 8
        remote(rsrc, rd, rt_s.at[k], rt_r.at[k], dev)
        remote(src, td, tok_s.at[k], tok_r.at[k], dev)

    send_block(tok_in, route_in, -1, z_up)
    send_block(tok_in, route_in, 1, z_dn)
    own_t, own_r = tslot(0)
    own_t[...] = tok_in[...]
    own_r[...] = route_in[...]

    tri = (
        lax.broadcasted_iota(jnp.int32, (128, 128), 0) < lax.broadcasted_iota(jnp.int32, (128, 128), 1)
    ).astype(F32).astype(BF)
    slot_iota = lax.broadcasted_iota(jnp.int32, (quarter, 128), 0).astype(F32)

    def gather_step(j):
        for off, dev, more in ((-j, z_up, j < 8), (j, z_dn, j < 7)):
            if off == 8:
                continue
            t, r = tslot(off)
            landed(r, rt_r.at[off + 8])
            landed(t, tok_r.at[off + 8])
            if more:
                send_block(t, r, off - 1 if off < 0 else off + 1, dev)

    def select(g):
        hits, weights = [], []
        for b in range(4):
            info = route[g, b].astype(F32)
            ids, nums = info[:8], info[8:]
            for o in range(NY):
                e = (((y + o) % NY) * NZ + z).astype(F32)
                hit = jnp.where(ids == e, 1.0, 0.0)
                hits.append(jnp.sum(hit, axis=0, keepdims=True))
                weights.append(jnp.sum(hit * nums, axis=0, keepdims=True) * (1.0 / 256.0))
        hit_all = jnp.concatenate(hits, axis=0)
        rank = jnp.dot(hit_all.astype(BF), tri, preferred_element_type=F32)
        code = jnp.where(hit_all > 0.5, rank, -1000.0)
        sel_cols = []
        for b in range(4):
            col, wcol = [], []
            for o in range(NY):
                r = b * NY + o
                same = slot_iota == code[r:r + 1] + float(b * CAP)
                col.append(jnp.where(same, 1.0, 0.0))
                wcol.append(jnp.where(same, weights[r], 0.0))
            wsel[g, :, b * 128:(b + 1) * 128] = jnp.concatenate(wcol, axis=0).astype(BF)
            sel_cols.append(jnp.concatenate(col, axis=0).astype(BF))
        sel = jnp.concatenate(sel_cols, axis=1)
        picked = jnp.dot(sel, tok[g], preferred_element_type=F32).astype(BF)
        for o in range(1, NY):
            ysend[g, pl.ds(o * quarter, quarter), :] = picked[o * quarter:(o + 1) * quarter]
            to = (NY - o) % NY
            remote(
                ysend.at[g, pl.ds(o * quarter, quarter), :],
                xfull.at[g, 0, pl.ds(to * quarter, quarter), :],
                y_s.at[g, to], y_r.at[g, to], y_at[o],
            )
        xfull[g, 0, pl.ds(0, quarter), :] = picked[:quarter]

    def rows_out(g):
        for o in range(1, NY):
            landed(xfull.at[g, 0, pl.ds(o * quarter, quarter), :], y_r.at[g, o])
        own = xfull.at[g, 0]
        remote(own, xfull.at[g, 6], x_s.at[g, 0], x_r.at[g, 0], x_up)
        remote(own, xfull.at[g, 2], x_s.at[g, 1], x_r.at[g, 1], x_dn)
        remote(own, xfull.at[g, 1], xc_s.at[g, 0], xc_r.at[g, 0], sib)

    def rows_forward(g):
        lo, hi = pl.ds(0, half), pl.ds(half, half)
        landed(xfull.at[g, 6], x_r.at[g, 0])
        remote(xfull.at[g, 6, lo, :], xfull.at[g, 4, lo, :], x_s.at[g, 2], x_r.at[g, 2], x_up)
        remote(xfull.at[g, 6], xfull.at[g, 7], xc_s.at[g, 1], xc_r.at[g, 1], sib)
        landed(xfull.at[g, 2], x_r.at[g, 1])
        remote(xfull.at[g, 2, hi, :], xfull.at[g, 4, hi, :], x_s.at[g, 3], x_r.at[g, 3], x_dn)
        remote(xfull.at[g, 2], xfull.at[g, 3], xc_s.at[g, 2], xc_r.at[g, 2], sib)

    def rows_last(g):
        lo, hi = pl.ds(0, half), pl.ds(half, half)
        landed(xfull.at[g, 4, lo, :], x_r.at[g, 2])
        landed(xfull.at[g, 4, hi, :], x_r.at[g, 3])
        remote(xfull.at[g, 4], xfull.at[g, 5], xc_s.at[g, 3], xc_r.at[g, 3], sib)

    state = {"w1": False, "w2": False}

    def first_matmul(g):
        if not state["w1"]:
            pltpu.make_async_copy(wgu, wgu, wg_sem).wait()
            state["w1"] = True
        for i, s in enumerate((1, 7, 3, 5)):
            landed(xfull.at[g, s], xc_r.at[g, i])
        acc1[...] = jnp.dot(xfull[g, 0], wgu[0], preferred_element_type=F32)

        def body(s, carry):
            acc1[...] += jnp.dot(xfull[g, s], wgu[s], preferred_element_type=F32)
            return carry

        lax.fori_loop(1, nsec, body, 0)
        lane = lax.broadcasted_iota(jnp.int32, (rows, 128), 1)
        parts = []
        for b in range(3):
            v = acc1[:, b * 128:(b + 1) * 128]
            other = pltpu.roll(v, 64, 1)
            low = lane < 64
            gate = jnp.where(low, v, other)
            up = jnp.where(low, other, v)
            parts.append(gate / (1.0 + jnp.exp(-gate)) * up)
        hx_send[g, :, 0:128] = jnp.where(lane < 64, parts[0], parts[1]).astype(BF)
        hx_send[g, :, 128:256] = parts[2].astype(BF)
        remote(
            hx_send.at[g, pl.ds(pl.multiple_of((1 - core) * half, half), half), :],
            hx_recv.at[g], hx_s.at[g], hx_r.at[g], sib,
        )

    mine = pl.ds(pl.multiple_of(core * half, half), half)
    mine_lo = pl.ds(pl.multiple_of(core * half, half // 2), half // 2)
    mine_hi = pl.ds(pl.multiple_of(core * half + half // 2, half // 2), half // 2)
    theirs = pl.ds(pl.multiple_of((1 - core) * half, half), half)

    def hidden_out(g):
        landed(hx_recv.at[g], hx_r.at[g])
        a = hx_send[g, mine, :].astype(F32)
        b = hx_recv[g].astype(F32)
        zero = core == 0
        first = jnp.where(zero, a, b)
        second = jnp.where(zero, b, a)
        lane = lax.broadcasted_iota(jnp.int32, (half, 128), 1)
        hfull[g, 0, mine, 0:128] = first[:, :128].astype(BF)
        hfull[g, 0, mine, 128:256] = jnp.where(lane < 64, first[:, 128:], second[:, 128:]).astype(BF)
        hfull[g, 0, mine, 256:384] = second[:, :128].astype(BF)
        own = hfull.at[g, 0, mine, :]
        remote(own, hfull.at[g, 3, mine, :], h_s.at[g, 0], h_r.at[g, 0], x_up)
        remote(own, hfull.at[g, 1, mine, :], h_s.at[g, 1], h_r.at[g, 1], x_dn)
        remote(own, hfull.at[g, 0, mine, :], hc_s.at[g, 0], hc_r.at[g, 0], sib)

    def hidden_forward(g):
        landed(hfull.at[g, 3, mine, :], h_r.at[g, 0])
        remote(hfull.at[g, 3, mine_lo, :], hfull.at[g, 2, mine_lo, :], h_s.at[g, 2], h_r.at[g, 2], x_up)
        remote(hfull.at[g, 3, mine, :], hfull.at[g, 3, mine, :], hc_s.at[g, 3], hc_r.at[g, 3], sib)
        landed(hfull.at[g, 1, mine, :], h_r.at[g, 1])
        remote(hfull.at[g, 1, mine_hi, :], hfull.at[g, 2, mine_hi, :], h_s.at[g, 3], h_r.at[g, 3], x_dn)
        remote(hfull.at[g, 1, mine, :], hfull.at[g, 1, mine, :], hc_s.at[g, 1], hc_r.at[g, 1], sib)

    def hidden_last(g):
        landed(hfull.at[g, 2, mine_lo, :], h_r.at[g, 2])
        landed(hfull.at[g, 2, mine_hi, :], h_r.at[g, 3])
        remote(hfull.at[g, 2, mine, :], hfull.at[g, 2, mine, :], hc_s.at[g, 2], hc_r.at[g, 2], sib)

    def second_matmul(g):
        if not state["w2"]:
            pltpu.make_async_copy(wd, wd, wd_sem).wait()
            state["w2"] = True
        for o in range(NX):
            landed(hfull.at[g, o, theirs, :], hc_r.at[g, o])
        acc2[...] = jnp.dot(hfull[g, 0], wd[0], preferred_element_type=F32)

        def body(o, carry):
            acc2[...] += jnp.dot(hfull[g, o], wd[o], preferred_element_type=F32)
            return carry

        lax.fori_loop(1, NX, body, 0)
        for o in range(1, NY):
            ret[g, pl.ds(o * quarter, quarter), :] = acc2[pl.ds(o * quarter, quarter), :].astype(BF)
            to = (NY - o) % NY
            remote(
                ret.at[g, pl.ds(o * quarter, quarter), :],
                back.at[g, pl.ds(to * quarter, quarter), :],
                b_s.at[g, to], b_r.at[g, to], y_at[o],
            )
        back[g, pl.ds(0, quarter), :] = acc2[pl.ds(0, quarter), :].astype(BF)

    def combine(g):
        for o in range(1, NY):
            landed(back.at[g, pl.ds(o * quarter, quarter), :], b_r.at[g, o])
        part[g] = lax.dot_general(
            wsel[g], back[g], (((0,), (0,)), ((), ())), preferred_element_type=F32
        )

    def share(off):
        g, i = PLACE[off]
        return part[g, pl.ds(i * 128, 128), :]

    def reduce_step(j):
        v = share(j - 8)
        if j > 0:
            landed(drecv.at[j - 1], d_r.at[j - 1])
            v = v + drecv[j - 1].astype(F32)
        dsend[j] = v.astype(BF)
        remote(dsend.at[j], drecv.at[j], d_s.at[j], d_r.at[j], z_dn)
        if j > 0:
            landed(urecv.at[j - 1], u_r.at[j - 1])
        if j < 7:
            v = share(7 - j)
            if j > 0:
                v = v + urecv[j - 1].astype(F32)
            usend[j] = v.astype(BF)
            remote(usend.at[j], urecv.at[j], u_s.at[j], u_r.at[j], z_up)

    steps = {
        "A": gather_step, "S": select, "Y": rows_out, "X": rows_forward, "Z": rows_last, "M": first_matmul,
        "H": hidden_out, "I": hidden_forward, "J": hidden_last, "N": second_matmul, "C": combine, "R": reduce_step,
    }
    for name in ORDER:
        steps[name[0]](int(name[1:]))

    landed(drecv.at[7], d_r.at[7])
    out_ref[...] = (share(0) + urecv[6].astype(F32) + drecv[7].astype(F32)).astype(BF)
    for c in pend:
        c.wait_send()


def shards(tokens, expert_ids, numerators, gate_up_weight, down_weight):
    route = jnp.concatenate([expert_ids.T, numerators.T], axis=0).astype(BF)
    feat = tokens.shape[1]
    rows = NY * 4 * CAP
    cols = gate_up_weight.shape[2]
    units = down_weight.shape[1] // NX
    dma = pltpu.SemaphoreType.DMA
    return pl.pallas_call(
        kernel,
        out_shape=jax.ShapeDtypeStruct(tokens.shape, BF),
        in_specs=[
            pl.BlockSpec(memory_space=pltpu.VMEM),
            pl.BlockSpec(memory_space=pltpu.VMEM),
            pl.BlockSpec(memory_space=pl.ANY),
            pl.BlockSpec(memory_space=pl.ANY),
        ],
        out_specs=pl.BlockSpec(memory_space=pltpu.VMEM),
        scratch_shapes=[
            pltpu.VMEM((4, 512, feat), BF),
            pltpu.VMEM((4, 4, 16, 128), BF),
            pltpu.VMEM((8, feat, cols), BF),
            pltpu.VMEM((NX, units, feat), BF),
            pltpu.VMEM((4, rows, 512), BF),
            pltpu.VMEM((4, rows, feat), BF),
            pltpu.VMEM((4, 8, rows, feat), BF),
            pltpu.VMEM((rows, cols), F32),
            pltpu.VMEM((4, rows, 256), BF),
            pltpu.VMEM((4, rows // 2, 256), BF),
            pltpu.VMEM((4, NX, rows, units), BF),
            pltpu.VMEM((rows, feat), F32),
            pltpu.VMEM((4, rows, feat), BF),
            pltpu.VMEM((4, rows, feat), BF),
            pltpu.VMEM((4, 512, feat), F32),
            pltpu.VMEM((8, 128, feat), BF),
            pltpu.VMEM((7, 128, feat), BF),
            pltpu.VMEM((8, 128, feat), BF),
            pltpu.VMEM((7, 128, feat), BF),
            dma, dma,
            dma((16,)), dma((16,)), dma((16,)), dma((16,)),
            dma((4, 4)), dma((4, 4)),
            dma((4, 4)), dma((4, 4)), dma((4, 4)), dma((4, 4)),
            dma((4,)), dma((4,)), dma((4, 4)), dma((4, 4)), dma((4, 4)), dma((4, 4)),
            dma((4, 4)), dma((4, 4)),
            dma((8,)), dma((8,)), dma((7,)), dma((7,)),
        ],
        compiler_params=pltpu.CompilerParams(
            collective_id=0, has_side_effects=True, vmem_limit_bytes=56 * 1024 * 1024
        ),
    )(tokens, route, gate_up_weight, down_weight)


def solution(mesh):
    in_specs = (
        P("expert", "section"),
        P("expert", None),
        P("expert", None),
        P("expert", None, "section"),
        P("expert", None, "section"),
    )
    out_specs = P("expert", "section")
    return jax.shard_map(shards, mesh=mesh, in_specs=in_specs, out_specs=out_specs, check_vma=False)
```

```python
import functools

import jax
import jax.numpy as jnp
from jax import lax
from jax.experimental import pallas as pl
from jax.experimental.pallas import tpu as pltpu
from jax.sharding import PartitionSpec as P

MESH = pl.DeviceIdType.MESH
BF = jnp.bfloat16
F32 = jnp.float32

NX, NY, NZ = 4, 4, 16
CAP = 20
AP, RP = 2, 4
GROUPS = ((6, -7, 7, -8), (4, -5, 5, -6), (2, -3, 3, -4), (0, -1, 1, -2))
PLACE = {off: (g, i) for g, offs in enumerate(GROUPS) for i, off in enumerate(offs)}
ORDER = (
    "A1.0", "A1.1", "A2.0", "A2.1", "S3", "A3.0", "A3.1", "A4.0", "Y3", "A4.1", "S2", "A5.1",
    "Y2", "A5.0", "A6.1", "A7.1", "X3", "A6.0", "S1", "X2", "A8.1", "A7.0", "Y1", "Z3",
    "A8.0", "S0", "Z2", "M2", "Y0", "M3", "X0", "X1", "H2", "Z0", "M0", "H0",
    "H3", "Z1", "M1", "I0", "H1", "J0", "I3", "N0", "I1", "I2", "J3", "C0",
    "R0.1", "R0.3", "J1", "R0.2", "R0.0", "J2", "N1", "R1.1", "R1.2", "R1.0", "R1.3", "N2",
    "C1", "R2.1", "R2.0", "R2.3", "R2.2", "N3", "R3.1", "R3.0", "C2", "R3.3", "R3.2", "R4.1",
    "R4.0", "R4.3", "R4.2", "C3", "R5.1", "R5.0", "R5.3", "R5.2", "R6.1", "R6.0", "R6.3", "R6.2",
    "R7.1", "R7.0", "R7.3", "R7.2",
)


def kernel(
    tok_in, route_in, wgu_hbm, wd_hbm, out_ref,
    tok, route, wgu, wd, wsel, ysend, xfull, acc1, hx_send, hx_recv, hfull, acc2, ret, back, part,
    dsend, usend, drecv, urecv,
    wg_sem, wd_sem, tok_s, tok_r, rt_s, rt_r, y_s, y_r, x_s, x_r, xc_s, xc_r,
    hx_s, hx_r, h_s, h_r, hc_s, hc_r, b_s, b_r, d_s, d_r, u_s, u_r,
):
    sec, exp = lax.axis_index("section"), lax.axis_index("expert")
    x, core = sec // 2, sec % 2
    y, z = exp // NZ, exp % NZ
    z_up = (sec, y * NZ + (z + 1) % NZ)
    z_dn = (sec, y * NZ + (z + NZ - 1) % NZ)
    y_at = [(sec, ((y + o) % NY) * NZ + z) for o in range(NY)]
    x_up = (((x + 1) % NX) * 2 + core, exp)
    x_dn = (((x + NX - 1) % NX) * 2 + core, exp)
    sib = (x * 2 + (1 - core), exp)
    peers = [z_up, z_dn, y_at[1], y_at[2], y_at[3], x_up, x_dn, sib]

    rows = NY * 4 * CAP
    quarter = 4 * CAP
    half = rows // 2
    feat = tok_in.shape[1]
    nsec = 2 * NX
    pend = []

    def remote(src, dst, ss, rs, dev):
        c = pltpu.make_async_remote_copy(
            src_ref=src, dst_ref=dst, send_sem=ss, recv_sem=rs, device_id=dev, device_id_type=MESH
        )
        c.start()
        pend.append(c)
        return c

    def landed(dst, rs):
        pltpu.make_async_remote_copy(
            src_ref=dst, dst_ref=dst, send_sem=rs, recv_sem=rs, device_id=sib, device_id_type=MESH
        ).wait_recv()

    for o in range(NX):
        for c in range(2):
            s = ((x + o) % NX) * 2 + (core + c) % 2
            pltpu.make_async_copy(
                wgu_hbm.at[0, pl.ds(pl.multiple_of(s * feat, feat), feat), :],
                wgu.at[o * 2 + c], wg_sem,
            ).start()
    units = wd_hbm.shape[1] // NX
    third = units // 6
    for o in range(NX):
        base = ((x + o) % NX) * units
        for frm, to, size in ((0, 0, 3), (5, 3, 1), (3, 4, 2)):
            pltpu.make_async_copy(
                wd_hbm.at[0, pl.ds(pl.multiple_of(base + frm * third, third), size * third), :],
                wd.at[o, pl.ds(to * third, size * third), :], wd_sem,
            ).start()

    barrier = pltpu.get_barrier_semaphore()
    for p in peers:
        pl.semaphore_signal(barrier, inc=1, device_id=p, device_id_type=MESH)
    pl.semaphore_wait(barrier, len(peers))

    def tslot(off):
        g, i = PLACE[off]
        return tok.at[g, pl.ds(i * 128, 128), :], route.at[g, i]

    def send_block(src, rsrc, off_there, dev, p):
        td, rd = tslot(off_there)
        k = off_there + 8
        cut = pl.ds(p * (128 // AP), 128 // AP)
        if p == 0:
            remote(rsrc, rd, rt_s.at[k], rt_r.at[k], dev)
        remote(src.at[cut, :], td.at[cut, :], tok_s.at[k, p], tok_r.at[k, p], dev)

    for p in range(AP):
        send_block(tok_in, route_in, -1, z_up, p)
        send_block(tok_in, route_in, 1, z_dn, p)
    own_t, own_r = tslot(0)
    own_t[...] = tok_in[...]
    own_r[...] = route_in[...]

    tri = (
        lax.broadcasted_iota(jnp.int32, (128, 128), 0) < lax.broadcasted_iota(jnp.int32, (128, 128), 1)
    ).astype(F32).astype(BF)
    slot_iota = lax.broadcasted_iota(jnp.int32, (quarter, 128), 0).astype(F32)

    def gather_step(j, p):
        cut = pl.ds(p * (128 // AP), 128 // AP)
        for off, dev, more in ((-j, z_up, j < 8), (j, z_dn, j < 7)):
            if off == 8:
                continue
            t, r = tslot(off)
            if p == 0:
                landed(r, rt_r.at[off + 8])
            landed(t.at[cut, :], tok_r.at[off + 8, p])
            if more:
                send_block(t, r, off - 1 if off < 0 else off + 1, dev, p)

    def select(g):
        hits, weights = [], []
        for b in range(4):
            info = route[g, b].astype(F32)
            ids, nums = info[:8], info[8:]
            for o in range(NY):
                e = (((y + o) % NY) * NZ + z).astype(F32)
                hit = jnp.where(ids == e, 1.0, 0.0)
                hits.append(jnp.sum(hit, axis=0, keepdims=True))
                weights.append(jnp.sum(hit * nums, axis=0, keepdims=True) * (1.0 / 256.0))
        hit_all = jnp.concatenate(hits, axis=0)
        rank = jnp.dot(hit_all.astype(BF), tri, preferred_element_type=F32)
        code = jnp.where(hit_all > 0.5, rank, -1000.0)
        sel_cols = []
        for b in range(4):
            col, wcol = [], []
            for o in range(NY):
                r = b * NY + o
                same = slot_iota == code[r:r + 1] + float(b * CAP)
                col.append(jnp.where(same, 1.0, 0.0))
                wcol.append(jnp.where(same, weights[r], 0.0))
            wsel[g, :, b * 128:(b + 1) * 128] = jnp.concatenate(wcol, axis=0).astype(BF)
            sel_cols.append(jnp.concatenate(col, axis=0).astype(BF))
        sel = jnp.concatenate(sel_cols, axis=1)
        picked = jnp.dot(sel, tok[g], preferred_element_type=F32).astype(BF)
        for o in range(1, NY):
            ysend[g, pl.ds(o * quarter, quarter), :] = picked[o * quarter:(o + 1) * quarter]
            to = (NY - o) % NY
            remote(
                ysend.at[g, pl.ds(o * quarter, quarter), :],
                xfull.at[g, 0, pl.ds(to * quarter, quarter), :],
                y_s.at[g, to], y_r.at[g, to], y_at[o],
            )
        xfull[g, 0, pl.ds(0, quarter), :] = picked[:quarter]

    def rows_out(g):
        for o in range(1, NY):
            landed(xfull.at[g, 0, pl.ds(o * quarter, quarter), :], y_r.at[g, o])
        own = xfull.at[g, 0]
        remote(own, xfull.at[g, 6], x_s.at[g, 0], x_r.at[g, 0], x_up)
        remote(own, xfull.at[g, 2], x_s.at[g, 1], x_r.at[g, 1], x_dn)
        remote(own, xfull.at[g, 1], xc_s.at[g, 0], xc_r.at[g, 0], sib)

    def rows_forward(g):
        lo, hi = pl.ds(0, half), pl.ds(half, half)
        landed(xfull.at[g, 6], x_r.at[g, 0])
        remote(xfull.at[g, 6, lo, :], xfull.at[g, 4, lo, :], x_s.at[g, 2], x_r.at[g, 2], x_up)
        remote(xfull.at[g, 6], xfull.at[g, 7], xc_s.at[g, 1], xc_r.at[g, 1], sib)
        landed(xfull.at[g, 2], x_r.at[g, 1])
        remote(xfull.at[g, 2, hi, :], xfull.at[g, 4, hi, :], x_s.at[g, 3], x_r.at[g, 3], x_dn)
        remote(xfull.at[g, 2], xfull.at[g, 3], xc_s.at[g, 2], xc_r.at[g, 2], sib)

    def rows_last(g):
        lo, hi = pl.ds(0, half), pl.ds(half, half)
        landed(xfull.at[g, 4, lo, :], x_r.at[g, 2])
        landed(xfull.at[g, 4, hi, :], x_r.at[g, 3])
        remote(xfull.at[g, 4], xfull.at[g, 5], xc_s.at[g, 3], xc_r.at[g, 3], sib)

    state = {"w1": False, "w2": False}

    def first_matmul(g):
        if not state["w1"]:
            pltpu.make_async_copy(wgu, wgu, wg_sem).wait()
            state["w1"] = True
        for i, s in enumerate((1, 7, 3, 5)):
            landed(xfull.at[g, s], xc_r.at[g, i])
        acc1[...] = jnp.dot(xfull[g, 0], wgu[0], preferred_element_type=F32)

        def body(s, carry):
            acc1[...] += jnp.dot(xfull[g, s], wgu[s], preferred_element_type=F32)
            return carry

        lax.fori_loop(1, nsec, body, 0)
        lane = lax.broadcasted_iota(jnp.int32, (rows, 128), 1)
        parts = []
        for b in range(3):
            v = acc1[:, b * 128:(b + 1) * 128]
            other = pltpu.roll(v, 64, 1)
            low = lane < 64
            gate = jnp.where(low, v, other)
            up = jnp.where(low, other, v)
            parts.append(gate / (1.0 + jnp.exp(-gate)) * up)
        hx_send[g, :, 0:128] = jnp.where(lane < 64, parts[0], parts[1]).astype(BF)
        hx_send[g, :, 128:256] = parts[2].astype(BF)
        remote(
            hx_send.at[g, pl.ds(pl.multiple_of((1 - core) * half, half), half), :],
            hx_recv.at[g], hx_s.at[g], hx_r.at[g], sib,
        )

    mine = pl.ds(pl.multiple_of(core * half, half), half)
    mine_lo = pl.ds(pl.multiple_of(core * half, half // 2), half // 2)
    mine_hi = pl.ds(pl.multiple_of(core * half + half // 2, half // 2), half // 2)
    theirs = pl.ds(pl.multiple_of((1 - core) * half, half), half)

    def hidden_out(g):
        landed(hx_recv.at[g], hx_r.at[g])
        a = hx_send[g, mine, :].astype(F32)
        b = hx_recv[g].astype(F32)
        zero = core == 0
        first = jnp.where(zero, a, b)
        second = jnp.where(zero, b, a)
        lane = lax.broadcasted_iota(jnp.int32, (half, 128), 1)
        hfull[g, 0, mine, 0:128] = first[:, :128].astype(BF)
        hfull[g, 0, mine, 128:256] = jnp.where(lane < 64, first[:, 128:], second[:, 128:]).astype(BF)
        hfull[g, 0, mine, 256:384] = second[:, :128].astype(BF)
        own = hfull.at[g, 0, mine, :]
        remote(own, hfull.at[g, 3, mine, :], h_s.at[g, 0], h_r.at[g, 0], x_up)
        remote(own, hfull.at[g, 1, mine, :], h_s.at[g, 1], h_r.at[g, 1], x_dn)
        remote(own, hfull.at[g, 0, mine, :], hc_s.at[g, 0], hc_r.at[g, 0], sib)

    def hidden_forward(g):
        landed(hfull.at[g, 3, mine, :], h_r.at[g, 0])
        remote(hfull.at[g, 3, mine_lo, :], hfull.at[g, 2, mine_lo, :], h_s.at[g, 2], h_r.at[g, 2], x_up)
        remote(hfull.at[g, 3, mine, :], hfull.at[g, 3, mine, :], hc_s.at[g, 3], hc_r.at[g, 3], sib)
        landed(hfull.at[g, 1, mine, :], h_r.at[g, 1])
        remote(hfull.at[g, 1, mine_hi, :], hfull.at[g, 2, mine_hi, :], h_s.at[g, 3], h_r.at[g, 3], x_dn)
        remote(hfull.at[g, 1, mine, :], hfull.at[g, 1, mine, :], hc_s.at[g, 1], hc_r.at[g, 1], sib)

    def hidden_last(g):
        landed(hfull.at[g, 2, mine_lo, :], h_r.at[g, 2])
        landed(hfull.at[g, 2, mine_hi, :], h_r.at[g, 3])
        remote(hfull.at[g, 2, mine, :], hfull.at[g, 2, mine, :], hc_s.at[g, 2], hc_r.at[g, 2], sib)

    def second_matmul(g):
        if not state["w2"]:
            pltpu.make_async_copy(wd, wd, wd_sem).wait()
            state["w2"] = True
        for o in range(NX):
            landed(hfull.at[g, o, theirs, :], hc_r.at[g, o])
        acc2[...] = jnp.dot(hfull[g, 0], wd[0], preferred_element_type=F32)

        def body(o, carry):
            acc2[...] += jnp.dot(hfull[g, o], wd[o], preferred_element_type=F32)
            return carry

        lax.fori_loop(1, NX, body, 0)
        for o in range(1, NY):
            ret[g, pl.ds(o * quarter, quarter), :] = acc2[pl.ds(o * quarter, quarter), :].astype(BF)
            to = (NY - o) % NY
            remote(
                ret.at[g, pl.ds(o * quarter, quarter), :],
                back.at[g, pl.ds(to * quarter, quarter), :],
                b_s.at[g, to], b_r.at[g, to], y_at[o],
            )
        back[g, pl.ds(0, quarter), :] = acc2[pl.ds(0, quarter), :].astype(BF)

    def combine(g):
        for o in range(1, NY):
            landed(back.at[g, pl.ds(o * quarter, quarter), :], b_r.at[g, o])
        part[g] = lax.dot_general(
            wsel[g], back[g], (((0,), (0,)), ((), ())), preferred_element_type=F32
        )

    def share(off, p):
        g, i = PLACE[off]
        return part[g, pl.ds(i * 128 + p * (128 // RP), 128 // RP), :]

    def reduce_step(j, p):
        cut = pl.ds(p * (128 // RP), 128 // RP)
        v = share(j - 8, p)
        if j > 0:
            landed(drecv.at[j - 1, cut, :], d_r.at[j - 1, p])
            v = v + drecv[j - 1, cut, :].astype(F32)
        dsend[j, cut, :] = v.astype(BF)
        remote(dsend.at[j, cut, :], drecv.at[j, cut, :], d_s.at[j, p], d_r.at[j, p], z_dn)
        if j > 0:
            landed(urecv.at[j - 1, cut, :], u_r.at[j - 1, p])
        if j < 7:
            v = share(7 - j, p)
            if j > 0:
                v = v + urecv[j - 1, cut, :].astype(F32)
            usend[j, cut, :] = v.astype(BF)
            remote(usend.at[j, cut, :], urecv.at[j, cut, :], u_s.at[j, p], u_r.at[j, p], z_up)

    def finish(p):
        cut = pl.ds(p * (128 // RP), 128 // RP)
        landed(drecv.at[7, cut, :], d_r.at[7, p])
        out_ref[cut, :] = (
            share(0, p) + urecv[6, cut, :].astype(F32) + drecv[7, cut, :].astype(F32)
        ).astype(BF)

    steps = {
        "A": gather_step, "S": select, "Y": rows_out, "X": rows_forward, "Z": rows_last, "M": first_matmul,
        "H": hidden_out, "I": hidden_forward, "J": hidden_last, "N": second_matmul, "C": combine, "R": reduce_step,
    }
    for name in ORDER:
        steps[name[0]](*map(int, name[1:].split(".")))
    for p in range(RP):
        finish(p)
    for c in pend:
        c.wait_send()


def shards(tokens, expert_ids, numerators, gate_up_weight, down_weight):
    route = jnp.concatenate([expert_ids.T, numerators.T], axis=0).astype(BF)
    feat = tokens.shape[1]
    rows = NY * 4 * CAP
    cols = gate_up_weight.shape[2]
    units = down_weight.shape[1] // NX
    dma = pltpu.SemaphoreType.DMA
    return pl.pallas_call(
        kernel,
        out_shape=jax.ShapeDtypeStruct(tokens.shape, BF),
        in_specs=[
            pl.BlockSpec(memory_space=pltpu.VMEM),
            pl.BlockSpec(memory_space=pltpu.VMEM),
            pl.BlockSpec(memory_space=pl.ANY),
            pl.BlockSpec(memory_space=pl.ANY),
        ],
        out_specs=pl.BlockSpec(memory_space=pltpu.VMEM),
        scratch_shapes=[
            pltpu.VMEM((4, 512, feat), BF),
            pltpu.VMEM((4, 4, 16, 128), BF),
            pltpu.VMEM((8, feat, cols), BF),
            pltpu.VMEM((NX, units, feat), BF),
            pltpu.VMEM((4, rows, 512), BF),
            pltpu.VMEM((4, rows, feat), BF),
            pltpu.VMEM((4, 8, rows, feat), BF),
            pltpu.VMEM((rows, cols), F32),
            pltpu.VMEM((4, rows, 256), BF),
            pltpu.VMEM((4, rows // 2, 256), BF),
            pltpu.VMEM((4, NX, rows, units), BF),
            pltpu.VMEM((rows, feat), F32),
            pltpu.VMEM((4, rows, feat), BF),
            pltpu.VMEM((4, rows, feat), BF),
            pltpu.VMEM((4, 512, feat), F32),
            pltpu.VMEM((8, 128, feat), BF),
            pltpu.VMEM((7, 128, feat), BF),
            pltpu.VMEM((8, 128, feat), BF),
            pltpu.VMEM((7, 128, feat), BF),
            dma, dma,
            dma((16, AP)), dma((16, AP)), dma((16,)), dma((16,)),
            dma((4, 4)), dma((4, 4)),
            dma((4, 4)), dma((4, 4)), dma((4, 4)), dma((4, 4)),
            dma((4,)), dma((4,)), dma((4, 4)), dma((4, 4)), dma((4, 4)), dma((4, 4)),
            dma((4, 4)), dma((4, 4)),
            dma((8, RP)), dma((8, RP)), dma((7, RP)), dma((7, RP)),
        ],
        compiler_params=pltpu.CompilerParams(
            collective_id=0, has_side_effects=True, vmem_limit_bytes=56 * 1024 * 1024
        ),
    )(tokens, route, gate_up_weight, down_weight)


def solution(mesh):
    in_specs = (
        P("expert", "section"),
        P("expert", None),
        P("expert", None),
        P("expert", None, "section"),
        P("expert", None, "section"),
    )
    out_specs = P("expert", "section")
    return jax.shard_map(shards, mesh=mesh, in_specs=in_specs, out_specs=out_specs, check_vma=False)
```

```python
import functools

import jax
import jax.numpy as jnp
from jax import lax
from jax.experimental import pallas as pl
from jax.experimental.pallas import tpu as pltpu
from jax.sharding import PartitionSpec as P

MESH = pl.DeviceIdType.MESH
BF = jnp.bfloat16
F32 = jnp.float32

NX, NY, NZ = 4, 4, 16
CAP = 20
DIRECT = ()
AP, RP = 2, 4
GROUPS = ((6, -7, 7, -8), (4, -5, 5, -6), (2, -3, 3, -4), (0, -1, 1, -2))
PLACE = {off: (g, i) for g, offs in enumerate(GROUPS) for i, off in enumerate(offs)}
ORDER = (
    "A1.0", "A1.1", "A2.0", "A2.1", "S3", "Y3.0", "A3.0", "A3.1", "X3.0", "A4.0", "Y3.1", "Y3.2",
    "A4.1", "Y3.3", "S2", "A5.0", "X3.1", "Y2.0", "A5.1", "X3.2", "A6.0", "Y2.1", "A6.1", "S1",
    "Y1.0", "X2.0", "A7.0", "Z3.2", "A7.1", "X3.3", "Y1.2", "X2.1", "Y1.3", "A8.0", "A8.1", "S0",
    "Y0.0", "X1.0", "X1.2", "Y0.2", "Z3.3", "Z2.0", "Z2.1", "Y0.3", "Y0.1", "X0.0", "M3.1", "X0.2",
    "X0.3", "Y1.1", "X1.3", "M2.0", "X0.1", "Y2.2", "Y2.3", "Z0.2", "Z0.0", "Z0.3", "Z3.1", "M0.1",
    "Z0.1", "H0.1", "X1.1", "M0.0", "Z1.2", "X2.2", "Z1.3", "H0.0", "M1.1", "Z1.0", "I0.1", "Z1.1",
    "H1.1", "M1.0", "X2.3", "I0.0", "H1.0", "Z2.2", "H3.1", "J0.1", "I1.1", "N0.1", "H2.0", "J0.0",
    "Z2.3", "Z3.0", "N0.0", "I1.0", "M2.1", "J1.1", "H2.1", "N1.1", "J1.0", "C0", "R0.1", "R0.2",
    "N1.0", "R0.3", "R0.0", "I2.1", "M3.0", "R1.1", "I2.0", "I3.1", "R1.2", "H3.0", "R1.3", "J2.1",
    "R1.0", "C1", "N2.1", "R2.1", "J2.0", "R2.2", "J3.1", "R2.3", "N2.0", "R2.0", "I3.0", "R3.1",
    "R3.2", "R3.3", "N3.1", "R3.0", "C2", "R4.1", "J3.0", "R4.2", "R4.3", "N3.0", "R4.0", "R5.1",
    "R5.2", "R5.3", "R5.0", "C3", "R6.1", "R6.2", "R6.3", "R6.0", "R7.1", "R7.2", "R7.3", "R7.0",
)


def kernel(
    tok_in, ids_in, nums_in, wgu_hbm, wd_hbm, out_ref,
    tok, route, wgu, wd, wsel, ysend, xfull, acc1, hx_send, hx_recv, hfull, acc2, ret, back, part,
    dsend, usend, drecv, urecv,
    wg_sem, wd_sem, tok_s, tok_r, rt_s, rt_r, y_s, y_r, x_s, x_r, xc_s, xc_r,
    hx_s, hx_r, h_s, h_r, hc_s, hc_r, b_s, b_r, d_s, d_r, u_s, u_r,
):
    sec, exp = lax.axis_index("section"), lax.axis_index("expert")
    x, core = sec // 2, sec % 2
    y, z = exp // NZ, exp % NZ
    z_up = (sec, y * NZ + (z + 1) % NZ)
    z_dn = (sec, y * NZ + (z + NZ - 1) % NZ)
    y_at = [(sec, ((y + o) % NY) * NZ + z) for o in range(NY)]
    x_up = (((x + 1) % NX) * 2 + core, exp)
    x_dn = (((x + NX - 1) % NX) * 2 + core, exp)
    sib = (x * 2 + (1 - core), exp)
    x_far = (((x + 2) % NX) * 2 + core, exp)
    peers = [z_up, z_dn, y_at[1], y_at[2], y_at[3], x_up, x_dn, sib] + ([x_far] if DIRECT else [])

    rows = NY * 4 * CAP
    quarter = 4 * CAP
    half = rows // 2
    feat = tok_in.shape[1]
    nsec = 2 * NX
    pend = []

    def remote(src, dst, ss, rs, dev):
        c = pltpu.make_async_remote_copy(
            src_ref=src, dst_ref=dst, send_sem=ss, recv_sem=rs, device_id=dev, device_id_type=MESH
        )
        c.start()
        pend.append(c)
        return c

    def landed(dst, rs):
        pltpu.make_async_remote_copy(
            src_ref=dst, dst_ref=dst, send_sem=rs, recv_sem=rs, device_id=sib, device_id_type=MESH
        ).wait_recv()

    for o in range(NX):
        for c in range(2):
            s = ((x + o) % NX) * 2 + (core + c) % 2
            pltpu.make_async_copy(
                wgu_hbm.at[0, pl.ds(pl.multiple_of(s * feat, feat), feat), :],
                wgu.at[o * 2 + c], wg_sem,
            ).start()
    units = wd_hbm.shape[1] // NX
    third = units // 6
    for o in range(NX):
        base = ((x + o) % NX) * units
        for frm, to, size in ((0, 0, 3), (5, 3, 1), (3, 4, 2)):
            pltpu.make_async_copy(
                wd_hbm.at[0, pl.ds(pl.multiple_of(base + frm * third, third), size * third), :],
                wd.at[o, pl.ds(to * third, size * third), :], wd_sem,
            ).start()

    barrier = pltpu.get_barrier_semaphore()
    for p in peers:
        pl.semaphore_signal(barrier, inc=1, device_id=p, device_id_type=MESH)
    pl.semaphore_wait(barrier, len(peers))

    def tslot(off):
        g, i = PLACE[off]
        return tok.at[g, pl.ds(i * 128, 128), :], route.at[g, i]

    def send_block(src, rsrc, off_there, dev, p):
        td, rd = tslot(off_there)
        k = off_there + 8
        cut = pl.ds(p * (128 // AP), 128 // AP)
        if p == 0:
            remote(rsrc, rd, rt_s.at[k], rt_r.at[k], dev)
        remote(src.at[cut, :], td.at[cut, :], tok_s.at[k, p], tok_r.at[k, p], dev)

    own_t, own_r = tslot(0)
    own_r[...] = jnp.concatenate([ids_in[...], nums_in[...]], axis=0).astype(F32).astype(BF)
    for p in range(AP):
        send_block(tok_in, own_r, -1, z_up, p)
        send_block(tok_in, own_r, 1, z_dn, p)
    own_t[...] = tok_in[...]

    tri = (
        lax.broadcasted_iota(jnp.int32, (128, 128), 0) < lax.broadcasted_iota(jnp.int32, (128, 128), 1)
    ).astype(F32).astype(BF)
    slot_iota = lax.broadcasted_iota(jnp.int32, (quarter, 128), 0).astype(F32)

    def gather_step(j, p):
        cut = pl.ds(p * (128 // AP), 128 // AP)
        for off, dev, more in ((-j, z_up, j < 8), (j, z_dn, j < 7)):
            if off == 8:
                continue
            t, r = tslot(off)
            if p == 0:
                landed(r, rt_r.at[off + 8])
            landed(t.at[cut, :], tok_r.at[off + 8, p])
            if more:
                send_block(t, r, off - 1 if off < 0 else off + 1, dev, p)

    def select(g):
        hits, weights = [], []
        for b in range(4):
            info = route[g, b].astype(F32)
            ids, nums = info[:8], info[8:]
            for o in range(NY):
                e = (((y + o) % NY) * NZ + z).astype(F32)
                hit = jnp.where(ids == e, 1.0, 0.0)
                hits.append(jnp.sum(hit, axis=0, keepdims=True))
                weights.append(jnp.sum(hit * nums, axis=0, keepdims=True) * (1.0 / 256.0))
        hit_all = jnp.concatenate(hits, axis=0)
        rank = jnp.dot(hit_all.astype(BF), tri, preferred_element_type=F32)
        code = jnp.where(hit_all > 0.5, rank, -1000.0)
        sel_cols = []
        for b in range(4):
            col, wcol = [], []
            for o in range(NY):
                r = b * NY + o
                same = slot_iota == code[r:r + 1] + float(b * CAP)
                col.append(jnp.where(same, 1.0, 0.0))
                wcol.append(jnp.where(same, weights[r], 0.0))
            wsel[g, :, b * 128:(b + 1) * 128] = jnp.concatenate(wcol, axis=0).astype(BF)
            sel_cols.append(jnp.concatenate(col, axis=0).astype(BF))
        sel = jnp.concatenate(sel_cols, axis=1)
        picked = jnp.dot(sel, tok[g], preferred_element_type=F32).astype(BF)
        for o in (2, 1, 3):
            ysend[g, pl.ds(o * quarter, quarter), :] = picked[o * quarter:(o + 1) * quarter]
            to = (NY - o) % NY
            remote(
                ysend.at[g, pl.ds(o * quarter, quarter), :],
                xfull.at[g, 0, pl.ds(to * quarter, quarter), :],
                y_s.at[g, to], y_r.at[g, to], y_at[o],
            )
        xfull[g, 0, pl.ds(0, quarter), :] = picked[:quarter]

    def piece(q):
        return pl.ds(q * quarter, quarter)

    def rows_out(g, q):
        if q:
            landed(xfull.at[g, 0, piece(q), :], y_r.at[g, q])
        own = xfull.at[g, 0, piece(q), :]
        remote(own, xfull.at[g, 6, piece(q), :], x_s.at[g, 0, q], x_r.at[g, 0, q], x_up)
        remote(own, xfull.at[g, 2, piece(q), :], x_s.at[g, 1, q], x_r.at[g, 1, q], x_dn)
        remote(own, xfull.at[g, 1, piece(q), :], xc_s.at[g, 0, q], xc_r.at[g, 0, q], sib)

    def rows_forward(g, q):
        low, high = xfull.at[g, 6, piece(q), :], xfull.at[g, 2, piece(q), :]
        landed(low, x_r.at[g, 0, q])
        landed(high, x_r.at[g, 1, q])
        far = xfull.at[g, 4, piece(q), :]
        if q < 2:
            remote(low, far, x_s.at[g, 2, q], x_r.at[g, 2, q], x_up)
        else:
            remote(high, far, x_s.at[g, 2, q], x_r.at[g, 2, q], x_dn)
        remote(low, xfull.at[g, 7, piece(q), :], xc_s.at[g, 1, q], xc_r.at[g, 1, q], sib)
        remote(high, xfull.at[g, 3, piece(q), :], xc_s.at[g, 2, q], xc_r.at[g, 2, q], sib)

    def rows_last(g, q):
        landed(xfull.at[g, 4, piece(q), :], x_r.at[g, 2, q])
        remote(
            xfull.at[g, 4, piece(q), :], xfull.at[g, 5, piece(q), :], xc_s.at[g, 3, q], xc_r.at[g, 3, q], sib
        )

    state = {"w1": False, "w2": False}

    def first_matmul(g, h):
        if not state["w1"]:
            pltpu.make_async_copy(wgu, wgu, wg_sem).wait()
            state["w1"] = True
        for q in (2 * h, 2 * h + 1):
            for i, s in enumerate((1, 7, 3, 5)):
                landed(xfull.at[g, s, piece(q), :], xc_r.at[g, i, q])
        span = pl.ds(h * half, half)
        acc1[...] = jnp.dot(xfull[g, 0, span, :], wgu[0], preferred_element_type=F32)

        def body(s, carry):
            acc1[...] += jnp.dot(xfull[g, s, span, :], wgu[s], preferred_element_type=F32)
            return carry

        lax.fori_loop(1, nsec, body, 0)
        lane = lax.broadcasted_iota(jnp.int32, (half, 128), 1)
        parts = []
        for b in range(3):
            v = acc1[:, b * 128:(b + 1) * 128]
            other = pltpu.roll(v, 64, 1)
            low = lane < 64
            gate = jnp.where(low, v, other)
            up = jnp.where(low, other, v)
            parts.append(gate / (1.0 + jnp.exp(-gate)) * up)
        hx_send[g, span, 0:128] = jnp.where(lane < 64, parts[0], parts[1]).astype(BF)
        hx_send[g, span, 128:256] = parts[2].astype(BF)
        remote(hx_send.at[g, owned(h, 1 - core), :], hx_recv.at[g, h], hx_s.at[g, h], hx_r.at[g, h], sib)

    def owned(h, c):
        return pl.ds(pl.multiple_of(h * half + c * quarter, quarter), quarter)

    def hidden_out(g, h):
        landed(hx_recv.at[g, h], hx_r.at[g, h])
        mine = owned(h, core)
        a = hx_send[g, mine, :].astype(F32)
        b = hx_recv[g, h].astype(F32)
        zero = core == 0
        first = jnp.where(zero, a, b)
        second = jnp.where(zero, b, a)
        lane = lax.broadcasted_iota(jnp.int32, (quarter, 128), 1)
        hfull[g, 0, mine, 0:128] = first[:, :128].astype(BF)
        hfull[g, 0, mine, 128:256] = jnp.where(lane < 64, first[:, 128:], second[:, 128:]).astype(BF)
        hfull[g, 0, mine, 256:384] = second[:, :128].astype(BF)
        own = hfull.at[g, 0, mine, :]
        if g in DIRECT:
            remote(own, hfull.at[g, 2, mine, :], h_s.at[g, 2, h], h_r.at[g, 2, h], x_far)
        remote(own, hfull.at[g, 3, mine, :], h_s.at[g, 0, h], h_r.at[g, 0, h], x_up)
        remote(own, hfull.at[g, 1, mine, :], h_s.at[g, 1, h], h_r.at[g, 1, h], x_dn)
        remote(own, hfull.at[g, 0, mine, :], hc_s.at[g, 0, h], hc_r.at[g, 0, h], sib)

    def hidden_forward(g, h):
        mine = owned(h, core)
        low, high, far = hfull.at[g, 3, mine, :], hfull.at[g, 1, mine, :], hfull.at[g, 2, mine, :]
        landed(low, h_r.at[g, 0, h])
        landed(high, h_r.at[g, 1, h])
        if g not in DIRECT:
            if h == 0:
                remote(low, far, h_s.at[g, 2, h], h_r.at[g, 2, h], x_up)
            else:
                remote(high, far, h_s.at[g, 2, h], h_r.at[g, 2, h], x_dn)
        remote(low, low, hc_s.at[g, 3, h], hc_r.at[g, 3, h], sib)
        remote(high, high, hc_s.at[g, 1, h], hc_r.at[g, 1, h], sib)

    def hidden_last(g, h):
        far = hfull.at[g, 2, owned(h, core), :]
        landed(far, h_r.at[g, 2, h])
        remote(far, far, hc_s.at[g, 2, h], hc_r.at[g, 2, h], sib)

    def second_matmul(g, h):
        if not state["w2"]:
            pltpu.make_async_copy(wd, wd, wd_sem).wait()
            state["w2"] = True
        theirs = owned(h, 1 - core)
        for o in range(NX):
            landed(hfull.at[g, o, theirs, :], hc_r.at[g, o, h])
        span = pl.ds(h * half, half)
        acc2[...] = jnp.dot(hfull[g, 0, span, :], wd[0], preferred_element_type=F32)

        def body(o, carry):
            acc2[...] += jnp.dot(hfull[g, o, span, :], wd[o], preferred_element_type=F32)
            return carry

        lax.fori_loop(1, NX, body, 0)
        for o in (2 * h, 2 * h + 1):
            done = acc2[pl.ds((o - 2 * h) * quarter, quarter), :].astype(BF)
            if o == 0:
                back[g, piece(0), :] = done
                continue
            ret[g, piece(o), :] = done
            to = NY - o
            remote(ret.at[g, piece(o), :], back.at[g, piece(to), :], b_s.at[g, to], b_r.at[g, to], y_at[o])

    def combine(g):
        for o in range(1, NY):
            landed(back.at[g, pl.ds(o * quarter, quarter), :], b_r.at[g, o])
        part[g] = lax.dot_general(
            wsel[g], back[g], (((0,), (0,)), ((), ())), preferred_element_type=F32
        )

    def share(off, p):
        g, i = PLACE[off]
        return part[g, pl.ds(i * 128 + p * (128 // RP), 128 // RP), :]

    def reduce_step(j, p):
        cut = pl.ds(p * (128 // RP), 128 // RP)
        v = share(j - 8, p)
        if j > 0:
            landed(drecv.at[j - 1, cut, :], d_r.at[j - 1, p])
            v = v + drecv[j - 1, cut, :].astype(F32)
        dsend[j, cut, :] = v.astype(BF)
        remote(dsend.at[j, cut, :], drecv.at[j, cut, :], d_s.at[j, p], d_r.at[j, p], z_dn)
        if j > 0:
            landed(urecv.at[j - 1, cut, :], u_r.at[j - 1, p])
        if j < 7:
            v = share(7 - j, p)
            if j > 0:
                v = v + urecv[j - 1, cut, :].astype(F32)
            usend[j, cut, :] = v.astype(BF)
            remote(usend.at[j, cut, :], urecv.at[j, cut, :], u_s.at[j, p], u_r.at[j, p], z_up)

    def finish(p):
        cut = pl.ds(p * (128 // RP), 128 // RP)
        landed(drecv.at[7, cut, :], d_r.at[7, p])
        out_ref[cut, :] = (
            share(0, p) + urecv[6, cut, :].astype(F32) + drecv[7, cut, :].astype(F32)
        ).astype(BF)

    steps = {
        "A": gather_step, "S": select, "Y": rows_out, "X": rows_forward, "Z": rows_last, "M": first_matmul,
        "H": hidden_out, "I": hidden_forward, "J": hidden_last, "N": second_matmul, "C": combine, "R": reduce_step,
    }
    for name in ORDER:
        steps[name[0]](*map(int, name[1:].split(".")))
    for p in range(RP):
        finish(p)
    for c in pend:
        c.wait_send()


def shards(tokens, expert_ids, numerators, gate_up_weight, down_weight):
    feat = tokens.shape[1]
    rows = NY * 4 * CAP
    cols = gate_up_weight.shape[2]
    units = down_weight.shape[1] // NX
    dma = pltpu.SemaphoreType.DMA
    return pl.pallas_call(
        kernel,
        out_shape=jax.ShapeDtypeStruct(tokens.shape, BF),
        in_specs=[
            pl.BlockSpec(memory_space=pltpu.VMEM),
            pl.BlockSpec(memory_space=pltpu.VMEM),
            pl.BlockSpec(memory_space=pltpu.VMEM),
            pl.BlockSpec(memory_space=pl.ANY),
            pl.BlockSpec(memory_space=pl.ANY),
        ],
        out_specs=pl.BlockSpec(memory_space=pltpu.VMEM),
        scratch_shapes=[
            pltpu.VMEM((4, 512, feat), BF),
            pltpu.VMEM((4, 4, 16, 128), BF),
            pltpu.VMEM((8, feat, cols), BF),
            pltpu.VMEM((NX, units, feat), BF),
            pltpu.VMEM((4, rows, 512), BF),
            pltpu.VMEM((4, rows, feat), BF),
            pltpu.VMEM((4, 8, rows, feat), BF),
            pltpu.VMEM((rows // 2, cols), F32),
            pltpu.VMEM((4, rows, 256), BF),
            pltpu.VMEM((4, 2, rows // 4, 256), BF),
            pltpu.VMEM((4, NX, rows, units), BF),
            pltpu.VMEM((rows // 2, feat), F32),
            pltpu.VMEM((4, rows, feat), BF),
            pltpu.VMEM((4, rows, feat), BF),
            pltpu.VMEM((4, 512, feat), F32),
            pltpu.VMEM((8, 128, feat), BF),
            pltpu.VMEM((7, 128, feat), BF),
            pltpu.VMEM((8, 128, feat), BF),
            pltpu.VMEM((7, 128, feat), BF),
            dma, dma,
            dma((16, AP)), dma((16, AP)), dma((16,)), dma((16,)),
            dma((4, 4)), dma((4, 4)),
            dma((4, 3, 4)), dma((4, 3, 4)), dma((4, 4, 4)), dma((4, 4, 4)),
            dma((4, 2)), dma((4, 2)), dma((4, 3, 2)), dma((4, 3, 2)), dma((4, 4, 2)), dma((4, 4, 2)),
            dma((4, 4)), dma((4, 4)),
            dma((8, RP)), dma((8, RP)), dma((7, RP)), dma((7, RP)),
        ],
        compiler_params=pltpu.CompilerParams(
            collective_id=0, has_side_effects=True, vmem_limit_bytes=56 * 1024 * 1024
        ),
    )(tokens, expert_ids.T, numerators.T, gate_up_weight, down_weight)


def solution(mesh):
    in_specs = (
        P("expert", "section"),
        P("expert", None),
        P("expert", None),
        P("expert", None, "section"),
        P("expert", None, "section"),
    )
    out_specs = P("expert", "section")
    return jax.shard_map(shards, mesh=mesh, in_specs=in_specs, out_specs=out_specs, check_vma=False)
```
